512 devices in a mesh: group: 8 (over y_hi, core), tensor: 64 (over y_lo, x, z).
Axes of the slice: x: 4, y: 8 (y_hi: 4, y_lo: 2; y = y_hi * 2 + y_lo), z: 8, core: 2. Of those that a mesh axis runs over, the one named last changes fastest.
Arguments:
- resid_in: bfloat16 [8, 256, 2880], P('group', 'tensor'), may hold values from -8 to 8
- queries: bfloat16 [8, 256, 4096], P('group', None, 'tensor'), may hold values from -100 to 100
- suffix_kv: bfloat16 [8, 256, 1024], P('group', 'tensor'), may hold values from -12 to 12
- prefix_kv: bfloat16 [8, 2048, 1024], P('group', 'tensor'), may hold values from -7.1875 to 7.1875
- block_map: int32 [8, 64], P('group', 'tensor'), may hold values from 0 to 63, each once within a row
- lengths: int32 [8, 2], P('group'), may hold values from 1 to 128, as said below
- sinks: float32 [64], P('tensor'), may hold values from 7 to 12
- w_out: bfloat16 [4096, 2880], P('tensor'), may hold values from -1 to 1
- mlp_gain: float32 [2880], replicated, may hold values from 1 to 6
- routes: int32 [256, 8, 4], P('tensor'), may hold values from 0 to 31, all different within a row; in each aligned block of 32 rows (0 to 31, 32 to 63, ..., all dimensions but the last counted through in order) at most 8 rows name the same one
- w_experts: bfloat16 [512, 2880, 720], P(('group', 'tensor')), may hold values from -0.109375 to 0.109375
Outputs:
- resid_out: bfloat16 [8, 256, 2880], P('group', 'tensor')
- expert_hidden: bfloat16 [512, 64, 4, 360], P(('group', 'tensor'))
The draws below stay inside these ranges and needn't reach their ends.
Inputs may be any that keep to these rules, and one draw needn't show every extreme that they name: `lengths`: each group has one request of exactly 128 slots. `block_map`: each group's row is a permutation of the 64 block numbers. `routes`: each token names 4 different experts. Within one aligned block of slots (c * 4 to c * 4 + 3, all groups) no expert is named more than 8 times, a bound that some block reaches.
All inputs are finite; a program needn't handle non-finite values.
Results may differ from the reference program's by a relative error of at most 0.025.
Values may be sent and summed in bfloat16 or wider, within the bound.
A program may use at most 64 MiB of HBM per device.

```python
import math
import jax
import jax.numpy as jnp
import numpy as np
from jax import lax

D = 2880
HEADS = 64
KVH = 8
HD = 64
EXPERTS = 32
TOPK = 4
REQS = 2
MAXLEN = 128
PBLK = 32
SLOTS = 256
TOK_DEV = 4
PREFIX = 2048
PIECES = 512
PPE = 8
COPIES = 2
PFF = 360
ROUTE_CAP = 8
SLOT_CAP = 4
N_GROUP = 8
N_TENSOR = 64


def draw_resid_in(key, part):
    key_base, key_rows, key_cols = jax.random.split(jax.random.fold_in(key, 11), 3)
    draw_shape = (N_GROUP, SLOTS, D)
    base_draw = jnp.clip(jax.random.normal(key_base, draw_shape, jnp.float32), -5.0, 5.0)
    row_scale = jnp.exp(jax.random.uniform(key_rows, (N_GROUP, SLOTS, 1), jnp.float32, 0.0, 1.15))
    col_scale = jnp.exp(jax.random.uniform(key_cols, (1, 1, D), jnp.float32, 0.0, 1.15))
    return (0.15 * base_draw * row_scale * col_scale).astype(jnp.bfloat16)


def draw_queries(key, part):
    key_base = jax.random.fold_in(jax.random.fold_in(key, 23), 0)
    draw_shape = (N_GROUP, SLOTS, HEADS * HD)
    base_draw = jnp.clip(jax.random.normal(key_base, draw_shape, jnp.float32), -6.0, 6.0)
    return (1.4 * base_draw).astype(jnp.bfloat16)


def draw_lengths(key, part):
    key_values, key_spot = jax.random.split(jax.random.fold_in(key, 37), 2)
    values = jax.random.randint(key_values, (N_GROUP, REQS), 1, MAXLEN + 1)
    full_spot = jax.random.randint(key_spot, (N_GROUP, 1), 0, REQS)
    return jnp.where(jnp.arange(REQS)[None, :] == full_spot, MAXLEN, values).astype(jnp.int32)


def shard_levels(key, dims, shards, least, high):
    gain, own = 1.0, jax.random.fold_in(key, 6)
    for position, blocks in shards:
        heights = jnp.exp(jax.random.uniform(jax.random.fold_in(own, position), (blocks,), jnp.float32, least / len(shards), high / len(shards)))
        gain = gain * jnp.repeat(heights, dims[position] // blocks).reshape([-1 if axis == position else 1 for axis in range(len(dims))])
    return gain


def routed_block(key, own, number, rows, count, top, reach, skew):
    order = jax.random.permutation(key, count)
    packed, ordinary = load_shares(count, rows * top, reach, skew, True), load_shares(count, rows * top, reach, skew, False)
    places = jnp.arange(count)

    def named(sizes, rotation):
        used = int((sizes > 0).sum())
        fixed = max(1, used // 4)
        moved = fixed + (places - fixed + rotation * (used - fixed)) % max(1, count - fixed)
        return jnp.zeros((count,), jnp.int32).at[order[jnp.where(places < fixed, places, moved)]].set(jnp.asarray(sizes, jnp.int32))

    sizes = jnp.where(number % 4 == 0, named(packed, number // 4), named(ordinary, number - number // 4 - 1))
    mixed = jax.random.permutation(jax.random.fold_in(own, 3), count)
    source_of, receiver = mixed[0:count // 2 * 2:2], mixed[1:count // 2 * 2:2]
    margin = jnp.minimum(sizes[source_of] - 1, reach - sizes[receiver]) // 2
    margin = jnp.where((source_of == order[0]) | (receiver == order[0]) | (sizes[receiver] == 0), 0, jnp.maximum(margin, 0))
    moved = jax.random.randint(jax.random.fold_in(own, 4), (count // 2,), 0, 1 << 20) % (margin + 1)
    sizes = sizes.at[source_of].add(-moved).at[receiver].add(moved)
    items = jnp.searchsorted(jnp.cumsum(sizes), jnp.arange(rows * top), side="right").astype(jnp.int32)
    listing = items.reshape(top, rows).T
    listing = listing[jax.random.permutation(jax.random.fold_in(own, 1), rows)]
    rotation = jax.random.randint(jax.random.fold_in(own, 2), (rows, 1), 0, top)
    return jnp.take_along_axis(listing, (jnp.arange(top)[None, :] + rotation) % top, axis=1)


def load_shares(count, total, bound, slope, full):
    portions = [(1 << 20) // math.isqrt(rank ** slope) + 1 for rank in range(1, count + 1)]
    largest = bound if full else min(bound, max(-(-total // count), total * portions[0] // sum(portions)))
    least = 1 if total - largest >= count - 1 else 0
    holding, surplus = [largest] + [least] * (count - 1), total - largest - least * (count - 1)
    while surplus > 0:
        free = [i for i in range(1, count) if holding[i] < largest] or [i for i in range(1, count) if holding[i] < bound]
        mass, remaining = sum([portions[i] for i in free]), surplus
        for i in free:
            more = min(bound - holding[i], max(1, remaining * portions[i] // mass), surplus)
            holding[i] = holding[i] + more
            surplus = surplus - more
    return np.array(holding)


def noise(rng, shape, width, reach, pieces=(), kind=jnp.bfloat16):
    values = jax.random.normal(rng, shape, jnp.float32) * width
    if len(pieces) > 0:
        values = shard_levels(rng, shape, pieces, -0.22, 0.18) * values
    return jnp.clip(values, min=-reach, max=reach).astype(kind)


def setup_inputs(seed: int = 0) -> dict:
    arg_keys = jax.random.split(jax.random.key(seed), 12)
    resid_in = draw_resid_in(jax.random.fold_in(arg_keys[11], 71), 0)
    queries = draw_queries(jax.random.fold_in(arg_keys[11], 71), 0)
    suffix_kv = noise(arg_keys[2], (N_GROUP, SLOTS, 2 * KVH * HD), 2.0, 12.0, ((0, 8), (1, 64)))
    prefix_kv = noise(arg_keys[3], (N_GROUP, PREFIX, 2 * KVH * HD), 1.2, 7.1875, ((0, 8), (1, 64)))
    block_map = jax.vmap(lambda own: jax.random.permutation(own, N_TENSOR))(jax.random.split(arg_keys[4], N_GROUP)).reshape((N_GROUP, N_TENSOR)).astype(jnp.int32)
    lengths = draw_lengths(jax.random.fold_in(arg_keys[11], 71), 0)
    sinks = jnp.clip(7.0 + 5.0 * jax.random.uniform(arg_keys[6], (HEADS,), jnp.float32) ** shard_levels(arg_keys[6], (HEADS,), ((0, 64),), -0.2, 0.2), 7.0, 12.0)
    w_out = noise(arg_keys[7], (HEADS * HD, D), (HD // 2) ** -0.5, 1.0, ((0, 64),))
    mlp_gain = jnp.clip(jnp.exp(jax.random.uniform(arg_keys[8], (D,), jnp.float32, math.log(1.0), math.log(6.0))), 1.0, 6.0)
    routes_keys = jax.random.split(jax.random.fold_in(arg_keys[9], 1), SLOTS * N_GROUP // (TOK_DEV * N_GROUP))
    routes_turns = jax.random.permutation(jax.random.fold_in(arg_keys[9], 3), SLOTS * N_GROUP // (TOK_DEV * N_GROUP))
    routes = jax.vmap(lambda own, number: routed_block(jax.random.fold_in(arg_keys[9], 2), own, number, TOK_DEV * N_GROUP, EXPERTS, TOPK, ROUTE_CAP, 2))(routes_keys, routes_turns).reshape((SLOTS, N_GROUP, TOPK))
    w_experts = noise(arg_keys[10], (PIECES, D, 2 * PFF), D ** -0.5, 0.109375, ((0, 512),))
    return {"resid_in": resid_in, "queries": queries, "suffix_kv": suffix_kv, "prefix_kv": prefix_kv, "block_map": block_map, "lengths": lengths, "sinks": sinks, "w_out": w_out, "mlp_gain": mlp_gain, "routes": routes, "w_experts": w_experts}


def rotate(values, positions):
    half_width = HD // 2
    frequency = jnp.power(150000.0, -2.0 * jnp.arange(half_width, dtype=jnp.float32) / HD)
    angles = positions[:, None] * frequency[None, :]
    cosine = jnp.cos(angles)[:, None, :]
    sine_part = jnp.sin(angles)[:, None, :]
    first_half = values[..., :half_width]
    second = values[..., half_width:]
    return jnp.concatenate([first_half * cosine - second * sine_part, second * cosine + first_half * sine_part], axis=-1)

def attend(group_queries, group_suffix, group_prefix, group_blocks, group_lengths, sinks):
    slot_ids = jnp.arange(SLOTS)
    slot_pos = (PREFIX + slot_ids % MAXLEN).astype(jnp.float32)
    row_ids = jnp.arange(PREFIX)
    prefix_pos = (jnp.take(group_blocks, row_ids // PBLK) * PBLK + row_ids % PBLK).astype(jnp.float32)
    repeat = HEADS // KVH
    query_rot = rotate(group_queries.astype(jnp.float32).reshape(SLOTS, HEADS, HD), slot_pos).astype(jnp.bfloat16)
    query_f = lax.optimization_barrier(query_rot).astype(jnp.float32).reshape(SLOTS, KVH, repeat, HD)
    suffix = group_suffix.reshape(SLOTS, 2, KVH, HD)
    key_rot = rotate(suffix[:, 0].astype(jnp.float32), slot_pos).astype(jnp.bfloat16)
    key_rot = lax.optimization_barrier(key_rot).astype(jnp.float32)
    suffix_vals = suffix[:, 1].astype(jnp.float32)
    prefix = group_prefix.reshape(PREFIX, 2, KVH, HD)
    prefix_keys = rotate(prefix[:, 0].astype(jnp.float32), prefix_pos).astype(jnp.bfloat16)
    prefix_keys = lax.optimization_barrier(prefix_keys).astype(jnp.float32)
    prefix_vals = prefix[:, 1].astype(jnp.float32)

    def one_block(block_pair):
        key_block, value_block = block_pair
        scores = 0.125 * jnp.einsum('sgrd,pgd->grsp', query_f, key_block)
        block_max = lax.optimization_barrier(jnp.max(scores, axis=-1))
        weights = jnp.exp(scores - block_max[..., None])
        total_sum = lax.optimization_barrier(jnp.sum(weights, axis=-1))
        rounded = lax.optimization_barrier(weights.astype(jnp.bfloat16)).astype(jnp.float32)
        mixed_sum = jnp.einsum('grsp,pgd->grsd', rounded, value_block)
        return (block_max, total_sum, mixed_sum)
    block_maxes, block_sums, block_mixes = lax.map(one_block, (prefix_keys.reshape(N_TENSOR, PBLK, KVH, HD), prefix_vals.reshape(N_TENSOR, PBLK, KVH, HD)))
    request = slot_ids // MAXLEN
    within = slot_ids % MAXLEN
    live_len = jnp.take(group_lengths, request)
    visible = (request[:, None] == request[None, :]) & (slot_ids[None, :] <= slot_ids[:, None]) & (within[None, :] < live_len[None, :])
    scores = 0.125 * jnp.einsum('sgrd,tgd->grst', query_f, key_rot)
    masked = jnp.where(visible, scores, -1e+30)
    suffix_max = lax.optimization_barrier(jnp.max(masked, axis=-1))
    weights = jnp.where(visible, jnp.exp(masked - suffix_max[..., None]), 0.0)
    suffix_sum = lax.optimization_barrier(jnp.sum(weights, axis=-1))
    rounded = lax.optimization_barrier(weights.astype(jnp.bfloat16)).astype(jnp.float32)
    suffix_mix = jnp.einsum('grst,tgd->grsd', rounded, suffix_vals)
    sink_logit = sinks.reshape(KVH, repeat)[:, :, None]
    overall_max = jnp.maximum(jnp.maximum(sink_logit, suffix_max), lax.optimization_barrier(jnp.max(block_maxes, axis=0)))
    suffix_scale = jnp.exp(suffix_max - overall_max)
    block_scales = jnp.exp(block_maxes - overall_max[None])
    denominator = jnp.exp(sink_logit - overall_max) + suffix_sum * suffix_scale + lax.optimization_barrier(jnp.sum(block_sums * block_scales, axis=0))
    numerator = suffix_mix * suffix_scale[..., None] + lax.optimization_barrier(jnp.sum(block_mixes * block_scales[..., None], axis=0))
    combined = numerator / denominator[..., None]
    return jnp.transpose(combined, (2, 0, 1, 3)).reshape(SLOTS, HEADS * HD).astype(jnp.bfloat16)

def reference(resid_in, queries, suffix_kv, prefix_kv, block_map, lengths, sinks, w_out, mlp_gain, routes, w_experts):
    results = []
    for group_index in range(N_GROUP):
        attended = attend(queries[group_index], suffix_kv[group_index], prefix_kv[group_index], block_map[group_index], lengths[group_index], sinks)
        projected = jnp.dot(attended, w_out, preferred_element_type=jnp.float32)
        results.append((resid_in[group_index].astype(jnp.float32) + projected).astype(jnp.bfloat16))
    resid_out = jnp.stack(results)
    widened = resid_out.astype(jnp.float32)
    normed = (widened * lax.rsqrt(lax.optimization_barrier(jnp.mean(widened * widened, axis=-1, keepdims=True)) + 1e-05) * mlp_gain).astype(jnp.bfloat16)
    flat_rows = normed.reshape(N_GROUP * SLOTS, D)
    pair_count = TOK_DEV * N_GROUP * TOPK
    named_experts = routes.reshape(N_TENSOR, pair_count)
    pair_ids = jnp.arange(pair_count)
    local_slot = pair_ids // (N_GROUP * TOPK)
    pair_group = pair_ids // TOPK % N_GROUP
    pair_row = pair_group[None, :] * SLOTS + jnp.arange(N_TENSOR)[:, None] * TOK_DEV + local_slot[None, :]
    onehot = (named_experts[:, :, None] == jnp.arange(EXPERTS)[None, None, :]).astype(jnp.int32)
    pair_rank = lax.optimization_barrier(jnp.sum((jnp.cumsum(onehot, axis=1) - 1) * onehot, axis=-1))
    matches = (named_experts[:, None, None, :] == jnp.arange(EXPERTS)[None, :, None, None]) & (pair_rank[:, None, None, :] == jnp.arange(ROUTE_CAP)[None, None, :, None])
    chosen = lax.optimization_barrier(jnp.sum(jnp.where(matches, pair_row[:, None, None, :], 0), axis=-1)).astype(jnp.int32)
    filled = jnp.any(matches, axis=-1)
    slot_rows = jnp.where(filled[..., None], jnp.take(flat_rows, chosen, axis=0), jnp.zeros((), jnp.bfloat16))
    tensor_copies = N_TENSOR // COPIES

    def one_piece(piece_item):
        piece_index, piece_weights = piece_item
        column = piece_index % N_TENSOR
        distinct = piece_index // N_TENSOR * tensor_copies + column % tensor_copies
        expert = (distinct // PPE).astype(jnp.int32)
        copy_index = (column // tensor_copies).astype(jnp.int32)
        row_block = jnp.take(slot_rows, expert, axis=1).reshape(N_TENSOR, SLOT_CAP, COPIES, D)
        row_block = jnp.take(row_block, copy_index, axis=2).reshape(N_TENSOR * SLOT_CAP, D)
        projected = jnp.dot(row_block, piece_weights, preferred_element_type=jnp.float32)
        gate_part = jnp.minimum(projected[:, :PFF], 7.0)
        up_part = jnp.clip(projected[:, PFF:], -7.0, 7.0)
        activated = (up_part + 1.0) * gate_part * jax.nn.sigmoid(1.702 * gate_part)
        return activated.astype(jnp.bfloat16).reshape(N_TENSOR, SLOT_CAP, PFF)
    expert_hidden = lax.map(one_piece, (jnp.arange(PIECES).astype(jnp.int32), w_experts))
    return (resid_out, expert_hidden)
```

```python
import jax
import jax.numpy as jnp
import numpy as np
from jax import lax
from jax.experimental import pallas as pl
from jax.experimental.pallas import tpu as pltpu
from jax.sharding import PartitionSpec as P

MESH = pl.DeviceIdType.MESH
F32 = jnp.float32
BF16 = jnp.bfloat16

D = 2880
LEFT = 1536
RIGHT = D - LEFT
PFF = 360
NG = 8
NA = 8
NZ = 8
TOK = 4
PBLK = 32
SBLK = 8
KVR = PBLK + SBLK
KEYS = NZ * NA * KVR
SLOTS = NA * NZ * TOK
ROWS = NA * TOK
PREFIX = NA * NZ * PBLK
MAXLEN = 128


def tables():
    freq = 150000.0 ** (-2.0 * np.arange(32) / 64)

    def pair(positions):
        angle = np.asarray(positions, np.float64)[:, None] * freq[None, :]
        cos, sin = np.ones((len(angle), 128)), np.zeros((len(angle), 128))
        cos[:, :32] = cos[:, 32:64] = np.cos(angle)
        sin[:, :32] = sin[:, 32:64] = np.sin(angle)
        return cos.astype(np.float32), sin.astype(np.float32)

    slot = PREFIX + np.arange(SLOTS) % MAXLEN
    qcos, qsin = pair(slot)
    bcos, bsin = pair(np.arange(NA * NZ) * PBLK)
    icos, isin = pair(np.arange(PBLK))
    scos = np.ones((32, SBLK, 128), np.float32)
    ssin = np.zeros((32, SBLK, 128), np.float32)
    scos[:, :TOK] = qcos[:128].reshape(32, TOK, 128)
    ssin[:, :TOK] = qsin[:128].reshape(32, TOK, 128)
    n = np.arange(KEYS)
    block, i = n // KVR, n % KVR
    owner = block % NA * NZ + block // NA
    slot_of = np.where(i < PBLK, -1, np.where(i < PBLK + TOK, owner * TOK + i - PBLK, 1 << 20))
    keys = np.zeros((8, KEYS), np.int32)
    keys[0] = slot_of
    return qcos, qsin, bcos, bsin, icos, isin, scos, ssin, keys


def iota(shape, dim):
    return lax.broadcasted_iota(jnp.int32, shape, dim)


def one_hot(cond):
    return jnp.where(cond, 1.0, 0.0).astype(BF16)


def dot(x, y):
    return jnp.dot(x, y, preferred_element_type=F32)


def kernel(
    q_ref, sfx_ref, pfx_ref, bm_ref, len_ref, sink_ref, resid_ref, gain_ref, routes_ref, wout_ref, wexp_ref,
    qcos_ref, qsin_ref, bcos_ref, bsin_ref, icos_ref, isin_ref, scos_ref, ssin_ref, keys_ref,
    ro_ref, hid_ref,
    wexp_v, wbuf, kvmsg, kvbuf, qmsg, qbuf, bias_ref, kvb, s_ref, p_ref, att_ref, rsmsg, rsbuf, tmp, stmp, gmsg, gbuf,
    dmsg, xbuf, xl, xr,
    wexp_sem, wloc_sem, kv_s, kv_r, kvz_s, kvz_r, q_s, q_r, w_s, w_r, wp_s, wp_r, rs_s, rs_r, g_s, g_r, d_s, d_r, x_s, x_r,
):
    g = lax.axis_index("group")
    t = lax.axis_index("tensor")
    a = t // NZ
    z = lax.rem(t, NZ)
    c = lax.rem(g, 2)
    zr = lax.rem(z + 1, NZ)
    zl = lax.rem(z + NZ - 1, NZ)
    mate = g + 1 - 2 * c

    def at_tensor(aa, zz):
        return {"tensor": aa * NZ + zz}

    def remote(src, dst, ssem, rsem, device):
        return pltpu.make_async_remote_copy(
            src_ref=src, dst_ref=dst, send_sem=ssem, recv_sem=rsem, device_id=device, device_id_type=MESH
        )

    wexp_copy = pltpu.make_async_copy(wexp_ref, wexp_v, wexp_sem)
    wexp_copy.start()
    wloc = [
        pltpu.make_async_copy(wout_ref.at[pl.ds(32 * i, 32), :], wbuf.at[2 * z + i], wloc_sem.at[i]) for i in range(2)
    ]
    for copy in wloc:
        copy.start()

    barrier = pltpu.get_barrier_semaphore()
    for k in range(1, 8):
        pl.semaphore_signal(barrier, inc=1, device_id=at_tensor(lax.rem(a + k, NA), z), device_id_type=MESH)
        pl.semaphore_signal(barrier, inc=1, device_id=at_tensor(a, lax.rem(z + k, NZ)), device_id_type=MESH)
        pl.semaphore_signal(barrier, inc=1, device_id={"group": lax.rem(g + k, NG)}, device_id_type=MESH)

    def pack(block, cos, sin):
        rows = block.shape[0]
        lane = iota((rows, 128), 1)
        sin = jnp.where(lane < 32, -sin, sin)
        heads = []
        for j in range(4):
            kb = block[:, 128 * j : 128 * j + 128]
            vb = block[:, 512 + 128 * j : 640 + 128 * j]
            for packed in (
                jnp.where(lane < 64, kb, pltpu.roll(vb, 64, 1)),
                jnp.where(lane < 64, pltpu.roll(kb, 64, 1), vb),
            ):
                swapped = jnp.where(lane < 32, pltpu.roll(packed, 96, 1), pltpu.roll(packed, 32, 1))
                heads.append(packed * cos + swapped * sin)
        return heads

    mine = iota((NA * NZ, 128), 0) == bm_ref[0, 0]
    cos_b = jnp.sum(jnp.where(mine, bcos_ref[...], 0.0), axis=0, keepdims=True)
    sin_b = jnp.sum(jnp.where(mine, bsin_ref[...], 0.0), axis=0, keepdims=True)
    cos_p = cos_b * icos_ref[...] - sin_b * isin_ref[...]
    sin_p = sin_b * icos_ref[...] + cos_b * isin_ref[...]
    stmp[...] = jnp.zeros_like(stmp)
    stmp[0:TOK, :] = sfx_ref[...].astype(F32)
    prefix_heads = pack(pfx_ref[...].astype(F32), cos_p, sin_p)
    quarter = lax.rem(t, 32)
    suffix_heads = pack(stmp[...], scos_ref[quarter], ssin_ref[quarter])
    for h in range(NA):
        kvmsg[h] = jnp.concatenate([prefix_heads[h], suffix_heads[h]], axis=0).astype(BF16)
    kvbuf[z * NA + a] = kvmsg[a]

    swap_row, swap_col = iota((SLOTS, SLOTS), 0), iota((SLOTS, SLOTS), 1)
    swapped_row = ((swap_row >> 2) & 7) * 32 + (swap_row >> 5) * 4 + (swap_row & 3)
    swap = one_hot(swapped_row == swap_col)
    ei, el = iota((64, 128), 0), iota((64, 128), 1)
    q = q_ref[...]
    straight = dot(q, one_hot(ei == el))
    crossed = dot(q, one_hot(((el < 32) & (ei == el + 32)) | ((el >= 32) & (ei == el - 32))))
    qlane = iota((SLOTS, 128), 1)
    rotated = straight * qcos_ref[...] + crossed * jnp.where(qlane < 32, -qsin_ref[...], qsin_ref[...])
    rotated = dot(swap, (rotated * 0.125).astype(BF16))
    sink = jnp.broadcast_to(sink_ref[0], (SLOTS, 128))
    s1 = sink.astype(BF16).astype(F32)
    s2 = (sink - s1).astype(BF16).astype(F32)
    s3 = (sink - s1) - s2
    rotated = jnp.where(qlane < 64, rotated, 0.0)
    rotated = jnp.where(qlane == 64, s1, jnp.where(qlane == 65, s2, jnp.where(qlane == 66, s3, rotated)))
    qmsg[...] = rotated.reshape(NZ, ROWS, 128).astype(BF16)
    qbuf[z] = qmsg[z]

    for copy in wloc:
        copy.wait()
    pl.semaphore_wait(barrier, 21)

    def kv_copy(k):
        peer = lax.rem(a + k, NA)
        return remote(kvmsg.at[peer], kvbuf.at[z * NA + a], kv_s.at[k], kv_r.at[a], at_tensor(peer, z))

    def q_copy(k):
        peer = lax.rem(z + k, NZ)
        return remote(qmsg.at[peer], qbuf.at[z], q_s.at[k], q_r.at[z], at_tensor(a, peer))

    for k in range(1, 8):
        kv_copy(k).start()
    for k in range(1, 8):
        q_copy(k).start()

    def kv_ring(direction, k):
        block = lax.rem(z - (k - 1) + NZ, NZ) if direction == 0 else lax.rem(z + (k - 1), NZ)
        first, count = (block * NA, NA) if k < 4 else (block * NA + 4 * direction, 4)
        ref = kvbuf.at[pl.ds(first, count)]
        peer = at_tensor(a, zr if direction == 0 else zl)
        return remote(ref, ref, kvz_s.at[direction, k - 1], kvz_r.at[direction, k - 1], peer)

    def kv_arrived(direction, k):
        block = lax.rem(z - k + NZ, NZ) if direction == 0 else lax.rem(z + k, NZ)
        first, count = (block * NA, NA) if k < 4 else (block * NA + 4 * direction, 4)
        ref = kvbuf.at[pl.ds(first, count)]
        peer = at_tensor(a, zr if direction == 0 else zl)
        return remote(ref, ref, kvz_s.at[direction, k - 1], kvz_r.at[direction, k - 1], peer)

    def w_ref(block, direction, k):
        index = 2 * block + c
        return wbuf.at[index] if k < 4 else wbuf.at[index, pl.ds(16 * direction, 16)]

    def w_ring(direction, k):
        block = lax.rem(z - (k - 1) + NZ, NZ) if direction == 0 else lax.rem(z + (k - 1), NZ)
        ref = w_ref(block, direction, k)
        peer = at_tensor(a, zr if direction == 0 else zl)
        return remote(ref, ref, w_s.at[direction, k - 1], w_r.at[direction, k - 1], peer)

    def w_arrived(direction, k):
        block = lax.rem(z - k + NZ, NZ) if direction == 0 else lax.rem(z + k, NZ)
        ref = w_ref(block, direction, k)
        peer = at_tensor(a, zr if direction == 0 else zl)
        return remote(ref, ref, w_s.at[direction, k - 1], w_r.at[direction, k - 1], peer)

    def w_pass(direction, k):
        block = lax.rem(z - k + NZ, NZ) if direction == 0 else lax.rem(z + k, NZ)
        ref = w_ref(block, direction, k)
        return remote(ref, ref, wp_s.at[direction, k - 1], wp_r.at[direction, k - 1], {"group": mate})

    def w_passed(direction, k):
        block = lax.rem(z - k + NZ, NZ) if direction == 0 else lax.rem(z + k, NZ)
        index = 2 * block + 1 - c
        ref = wbuf.at[index] if k < 4 else wbuf.at[index, pl.ds(16 * direction, 16)]
        return remote(ref, ref, wp_s.at[direction, k - 1], wp_r.at[direction, k - 1], {"group": mate})

    for direction in range(2):
        w_ring(direction, 1).start()

    key_slot = jnp.broadcast_to(keys_ref[0:1, :], (ROWS, KEYS))
    row = iota((ROWS, KEYS), 0)
    own_slot = (row >> 2) * 32 + z * 4 + (row & 3)
    live = jnp.where(own_slot < MAXLEN, len_ref[0, 0], len_ref[0, 1])
    visible = (key_slot < 0) | (
        ((key_slot >> 7) == (own_slot >> 7)) & (key_slot <= own_slot) & ((key_slot & 127) < live)
    )
    bias_ref[...] = jnp.where(visible, 0.0, -1e30)

    pr, pc = iota((64, 128), 0), iota((64, 128), 1)
    named = jnp.broadcast_to(routes_ref[...], (64, 128)) == 4 * g + ((pr >> 3) & 3)
    ui, uj = iota((128, 128), 0), iota((128, 128), 1)
    rank = dot(one_hot(named), one_hot(ui < uj))
    wanted = (2 * (pr & 3) + (pr >> 5)).astype(F32)
    hit = one_hot(named & (rank == wanted))
    ti, tj = iota((128, 64), 0), iota((128, 64), 1)
    source = one_hot(((tj >> 3) == ((ti >> 2) & 7)) & ((tj & 3) == (ti >> 5)))
    qr, qc = iota((64, 64), 0), iota((64, 64), 1)
    select = jnp.where(((qr >> 2) & 1) == ((qc >> 2) & 1), dot(hit, source), 0.0).astype(BF16)

    for k in range(1, 8):
        src = lax.rem(a + k, NA)
        remote(kvmsg.at[src], kvbuf.at[z * NA + src], kv_s.at[k], kv_r.at[src], at_tensor(src, z)).wait_recv()
    for direction in range(2):
        kv_ring(direction, 1).start()
    for k in range(1, 5):
        for direction in range(2):
            kv_arrived(direction, k).wait_recv()
            if k < 4:
                kv_ring(direction, k + 1).start()
        if k < 4:
            for direction in range(2):
                w_arrived(direction, k).wait_recv()
                w_ring(direction, k + 1).start()
                w_pass(direction, k).start()

    for k in range(1, 8):
        src = lax.rem(z + k, NZ)
        remote(qmsg.at[src], qbuf.at[src], q_s.at[k], q_r.at[src], at_tensor(a, src)).wait_recv()
    kvb[...] = kvbuf[...].astype(F32).reshape(KEYS, 128).astype(BF16)
    qf = qbuf[...].astype(F32).reshape(SLOTS, 128)
    sinks = jnp.sum(jnp.where((qlane >= 64) & (qlane < 67), qf, 0.0), axis=1, keepdims=True)
    qk = jnp.where(qlane < 64, qf, 0.0).astype(BF16)
    s_ref[...] = lax.dot_general(qk, kvb[...], (((1,), (1,)), ((), ())), preferred_element_type=F32)
    scales = []
    for h in range(NZ):
        rows = slice(ROWS * h, ROWS * h + ROWS)
        scores = s_ref[rows, :] + bias_ref[...]
        sink_h = sinks[rows]
        top = jnp.maximum(jnp.max(scores, axis=1, keepdims=True), sink_h)
        weights = jnp.exp(scores - top)
        scales.append(1.0 / (jnp.sum(weights, axis=1, keepdims=True) + jnp.exp(sink_h - top)))
        p_ref[rows, :] = weights.astype(BF16)
    mixed = dot(p_ref[...], kvb[...]) * jnp.concatenate(scales, axis=0)
    alane = iota((ROWS, 128), 1)
    for j in range(4):
        even, odd = mixed[64 * j : 64 * j + 32], mixed[64 * j + 32 : 64 * j + 64]
        att_ref[:, 128 * j : 128 * j + 128] = jnp.where(alane < 64, pltpu.roll(even, 64, 1), odd).astype(BF16)

    for direction in range(2):
        w_arrived(direction, 4).wait_recv()
        w_pass(direction, 4).start()
    for k in range(1, 5):
        for direction in range(2):
            w_passed(direction, k).wait_recv()

    di, dj = iota((64, ROWS), 0), iota((64, ROWS), 1)
    doubled = dot(one_hot(((di >> 3) * 4 + (di & 3)) == dj), att_ref[...]).astype(BF16)
    weights = wbuf[...].reshape(NZ * 64, D)
    left = dot(doubled, weights[:, :LEFT])
    right = dot(doubled, weights[:, LEFT:])
    half = (iota((64, RIGHT), 0) >> 2) & 1
    rsmsg[:, :, 0:RIGHT] = jnp.where(half == 0, left[:, :RIGHT], right).reshape(NA, 8, RIGHT).astype(BF16)
    rsmsg[:, :, RIGHT:LEFT] = left[:, RIGHT:].reshape(NA, 8, LEFT - RIGHT).astype(BF16)
    rsbuf[a] = rsmsg[a]

    def rs_copy(k):
        peer = lax.rem(a + k, NA)
        return remote(rsmsg.at[peer], rsbuf.at[a], rs_s.at[k], rs_r.at[a], at_tensor(peer, z))

    for k in range(1, 8):
        rs_copy(k).start()
    for k in range(1, 8):
        src = lax.rem(a + k, NA)
        remote(rsmsg.at[src], rsbuf.at[src], rs_s.at[k], rs_r.at[src], at_tensor(src, z)).wait_recv()

    total = rsbuf[0].astype(F32)
    for k in range(1, 8):
        total = total + rsbuf[k].astype(F32)
    tmp[...] = total
    resid = resid_ref[...].astype(F32)
    out_l = (resid[:, :LEFT] + tmp[0:TOK, :]).astype(BF16)
    out_r = (resid[:, LEFT:] + tmp[TOK:8, 0:RIGHT]).astype(BF16)
    ro_ref[:, 0:LEFT] = out_l
    ro_ref[:, LEFT:D] = out_r
    wide_l, wide_r = out_l.astype(F32), out_r.astype(F32)
    square = jnp.sum(wide_l * wide_l, axis=1, keepdims=True) + jnp.sum(wide_r * wide_r, axis=1, keepdims=True)
    scale = lax.rsqrt(square / D + 1e-05)
    tmp[...] = jnp.zeros_like(tmp)
    tmp[0:TOK, :] = wide_l * scale * gain_ref[:, 0:LEFT]
    tmp[TOK:8, 0:RIGHT] = wide_r * scale * gain_ref[:, LEFT:D]
    gmsg[...] = tmp[...].astype(BF16)
    gbuf[g] = gmsg[...]

    def g_copy(k):
        peer = lax.rem(g + k, NG)
        return remote(gmsg, gbuf.at[g], g_s.at[k], g_r.at[g], {"group": peer})

    for k in range(1, 8):
        g_copy(k).start()
    for k in range(1, 8):
        src = lax.rem(g + k, NG)
        remote(gmsg, gbuf.at[src], g_s.at[k], g_r.at[src], {"group": src}).wait_recv()

    pool = gbuf[...].astype(F32).reshape(64, LEFT).astype(BF16)
    dmsg[...] = dot(select, pool).reshape(NA, 8, LEFT).astype(BF16)
    xbuf[z * NA + a] = dmsg[a]

    def d_copy(k):
        peer = lax.rem(a + k, NA)
        return remote(dmsg.at[peer], xbuf.at[z * NA + a], d_s.at[k], d_r.at[a], at_tensor(peer, z))

    for k in range(1, 8):
        d_copy(k).start()

    def x_send(direction, k, j):
        block = lax.rem(z - (k - 1) + NZ, NZ) if direction == 0 else lax.rem(z + (k - 1), NZ)
        ref = xbuf.at[block * NA + j]
        peer = at_tensor(a, zr if direction == 0 else zl)
        return remote(ref, ref, x_s.at[direction, k - 1, j], x_r.at[direction, k - 1, j], peer)

    def x_arrived(direction, k, j):
        block = lax.rem(z - k + NZ, NZ) if direction == 0 else lax.rem(z + k, NZ)
        ref = xbuf.at[block * NA + j]
        peer = at_tensor(a, zr if direction == 0 else zl)
        return remote(ref, ref, x_s.at[direction, k - 1, j], x_r.at[direction, k - 1, j], peer)

    ri, rj = iota((64, 64), 0), iota((64, 64), 1)
    regroup = one_hot(rj == (((ri >> 2) & 7) * 8 + (ri >> 5) * 4 + (ri & 3)))

    def unpack(block):
        plane = xbuf[pl.ds(block * NA, NA)].astype(F32).reshape(64, LEFT).astype(BF16)
        split = dot(regroup, plane).astype(BF16)
        xl[block] = split[0:ROWS]
        xr[block] = split[ROWS:64, 0:RIGHT]

    for k in range(8):
        src = lax.rem(a + k, NA)
        if k > 0:
            remote(dmsg.at[src], xbuf.at[z * NA + src], d_s.at[k], d_r.at[src], at_tensor(src, z)).wait_recv()
        for direction in range(2):
            x_send(direction, 1, src).start()
    unpack(z)
    for k in range(1, 5):
        for i in range(8):
            for direction in range(2):
                if k < 4:
                    j = lax.rem(a + i, NA)
                    x_arrived(direction, k, j).wait_recv()
                    if k < 3:
                        x_send(direction, k + 1, j).start()
                elif i < 4:
                    x_arrived(direction, k, 4 * direction + i).wait_recv()
        if k == 3:
            for i in range(4):
                for direction in range(2):
                    x_send(direction, 4, 4 * direction + i).start()
        unpack(lax.rem(z - k + NZ, NZ))
        if k < 4:
            unpack(lax.rem(z + k, NZ))

    wexp_copy.wait()
    y = dot(xl[...].reshape(SLOTS, LEFT), wexp_v[0:LEFT, :]) + dot(xr[...].reshape(SLOTS, RIGHT), wexp_v[LEFT:D, :])
    gate = jnp.minimum(y[:, 0:PFF], 7.0)
    up = jnp.clip(y[:, PFF : 2 * PFF], -7.0, 7.0)
    hidden = ((up + 1.0) * gate * (1.0 / (1.0 + jnp.exp(-1.702 * gate)))).astype(BF16)
    hid_ref[...] = dot(swap, hidden).astype(BF16)

    for k in range(1, 8):
        kv_copy(k).wait_send()
        q_copy(k).wait_send()
        rs_copy(k).wait_send()
        g_copy(k).wait_send()
        d_copy(k).wait_send()
    for direction in range(2):
        for k in range(1, 5):
            kv_ring(direction, k).wait_send()
            w_ring(direction, k).wait_send()
            w_pass(direction, k).wait_send()
            for i in range(8 if k < 4 else 4):
                x_send(direction, k, i if k < 4 else 4 * direction + i).wait_send()


def local(resid_in, queries, suffix_kv, prefix_kv, block_map, lengths, sinks, w_out, mlp_gain, routes, w_experts):
    vmem = pl.BlockSpec(memory_space=pltpu.VMEM)
    smem = pl.BlockSpec(memory_space=pltpu.SMEM)
    hbm = pl.BlockSpec(memory_space=pl.ANY)
    constants = [jnp.asarray(x) for x in tables()]
    dma = pltpu.SemaphoreType.DMA
    resid_out, hidden = pl.pallas_call(
        kernel,
        name="layer",
        out_shape=(jax.ShapeDtypeStruct((TOK, D), BF16), jax.ShapeDtypeStruct((SLOTS, PFF), BF16)),
        in_specs=[vmem, vmem, vmem, smem, smem, smem, vmem, vmem, vmem, hbm, hbm] + [vmem] * len(constants),
        out_specs=(vmem, vmem),
        scratch_shapes=[
            pltpu.VMEM((D, 2 * PFF), BF16),
            pltpu.VMEM((2 * NZ, 32, D), BF16),
            pltpu.VMEM((NA, KVR, 128), BF16),
            pltpu.VMEM((NZ * NA, KVR, 128), BF16),
            pltpu.VMEM((NZ, ROWS, 128), BF16),
            pltpu.VMEM((NZ, ROWS, 128), BF16),
            pltpu.VMEM((ROWS, KEYS), F32),
            pltpu.VMEM((KEYS, 128), BF16),
            pltpu.VMEM((SLOTS, KEYS), F32),
            pltpu.VMEM((SLOTS, KEYS), BF16),
            pltpu.VMEM((ROWS, 512), BF16),
            pltpu.VMEM((NA, 8, LEFT), BF16),
            pltpu.VMEM((NA, 8, LEFT), BF16),
            pltpu.VMEM((8, LEFT), F32),
            pltpu.VMEM((SBLK, 1024), F32),
            pltpu.VMEM((8, LEFT), BF16),
            pltpu.VMEM((NG, 8, LEFT), BF16),
            pltpu.VMEM((NA, 8, LEFT), BF16),
            pltpu.VMEM((NZ * NA, 8, LEFT), BF16),
            pltpu.VMEM((NZ, ROWS, LEFT), BF16),
            pltpu.VMEM((NZ, ROWS, RIGHT), BF16),
            dma,
            dma((2,)),
            dma((8,)), dma((8,)),
            dma((2, 4)), dma((2, 4)),
            dma((8,)), dma((8,)),
            dma((2, 4)), dma((2, 4)),
            dma((2, 4)), dma((2, 4)),
            dma((8,)), dma((8,)),
            dma((8,)), dma((8,)),
            dma((8,)), dma((8,)),
            dma((2, 4, 8)), dma((2, 4, 8)),
        ],
        compiler_params=pltpu.CompilerParams(
            collective_id=0, has_side_effects=True, vmem_limit_bytes=60 * 1024 * 1024
        ),
    )(
        queries[0], suffix_kv[0], prefix_kv[0], block_map, lengths, sinks, resid_in[0], mlp_gain.reshape(1, D),
        routes.reshape(1, 128), w_out, w_experts[0], *constants,
    )
    return (resid_out[None], hidden.reshape(1, NA * NZ, TOK, PFF))


def solution(mesh):
    placed = (
        P("group", "tensor", None),
        P("group", None, "tensor"),
        P("group", "tensor", None),
        P("group", "tensor", None),
        P("group", "tensor"),
        P("group", None),
        P("tensor"),
        P("tensor", None),
        P(),
        P("tensor", None, None),
        P(("group", "tensor"), None, None),
    )
    return jax.shard_map(
        local,
        mesh=mesh,
        in_specs=placed,
        out_specs=(P("group", "tensor", None), P(("group", "tensor"), None, None, None)),
        check_vma=False,
    )
```

```python
import jax
import jax.numpy as jnp
import numpy as np
from jax import lax
from jax.experimental import pallas as pl
from jax.experimental.pallas import tpu as pltpu
from jax.sharding import PartitionSpec as P

MESH = pl.DeviceIdType.MESH
F32 = jnp.float32
BF16 = jnp.bfloat16

D = 2880
LEFT = 1536
RIGHT = D - LEFT
PFF = 360
NG = 8
NA = 8
NZ = 8
TOK = 4
PBLK = 32
SBLK = 8
KVR = PBLK + SBLK
KEYS = NZ * NA * KVR
SLOTS = NA * NZ * TOK
ROWS = NA * TOK
PREFIX = NA * NZ * PBLK
MAXLEN = 128


def tables():
    freq = 150000.0 ** (-2.0 * np.arange(32) / 64)

    def pair(positions):
        angle = np.asarray(positions, np.float64)[:, None] * freq[None, :]
        cos, sin = np.ones((len(angle), 128)), np.zeros((len(angle), 128))
        cos[:, :32] = cos[:, 32:64] = np.cos(angle)
        sin[:, :32] = sin[:, 32:64] = np.sin(angle)
        return cos.astype(np.float32), sin.astype(np.float32)

    slot = PREFIX + np.arange(SLOTS) % MAXLEN
    qcos, qsin = pair(slot)
    bcos, bsin = pair(np.arange(NA * NZ) * PBLK)
    icos, isin = pair(np.arange(PBLK))
    scos = np.ones((32, SBLK, 128), np.float32)
    ssin = np.zeros((32, SBLK, 128), np.float32)
    scos[:, :TOK] = qcos[:128].reshape(32, TOK, 128)
    ssin[:, :TOK] = qsin[:128].reshape(32, TOK, 128)
    n = np.arange(KEYS)
    block, i = n // KVR, n % KVR
    owner = block % NA * NZ + block // NA
    slot_of = np.where(i < PBLK, -1, np.where(i < PBLK + TOK, owner * TOK + i - PBLK, 1 << 20))
    keys = np.zeros((8, KEYS), np.int32)
    keys[0] = slot_of
    return qcos, qsin, bcos, bsin, icos, isin, scos, ssin, keys


def iota(shape, dim):
    return lax.broadcasted_iota(jnp.int32, shape, dim)


def one_hot(cond):
    return jnp.where(cond, 1.0, 0.0).astype(BF16)


def dot(x, y):
    return jnp.dot(x, y, preferred_element_type=F32)


def dot_t(x, y):
    return lax.dot_general(x, y, (((1,), (1,)), ((), ())), preferred_element_type=F32)


def kernel(
    q_ref, sfx_ref, pfx_ref, bm_ref, len_ref, sink_ref, resid_ref, gain_ref, routes_ref, wout_ref, wexp_ref,
    qcos_ref, qsin_ref, bcos_ref, bsin_ref, icos_ref, isin_ref, scos_ref, ssin_ref, keys_ref,
    ro_ref, hid_ref,
    wexp_v, wbuf, kvmsg, kvbuf, qmsg, qbuf, bias_ref, kvb, s_ref, p_ref, att_ref, rsmsg, rsbuf, tmp, stmp, gmsg, gbuf,
    dmsg, xbuf, xl, xr,
    wexp_sem, wloc_sem, kv_s, kv_r, kvz_s, kvz_r, q_s, q_r, w_s, w_r, wp_s, wp_r, rs_s, rs_r, g_s, g_r, d_s, d_r, x_s, x_r,
):
    g = lax.axis_index("group")
    t = lax.axis_index("tensor")
    a = t // NZ
    z = lax.rem(t, NZ)
    c = lax.rem(g, 2)
    zr = lax.rem(z + 1, NZ)
    zl = lax.rem(z + NZ - 1, NZ)
    mate = g + 1 - 2 * c

    def at_tensor(aa, zz):
        return {"tensor": aa * NZ + zz}

    def remote(src, dst, ssem, rsem, device):
        return pltpu.make_async_remote_copy(
            src_ref=src, dst_ref=dst, send_sem=ssem, recv_sem=rsem, device_id=device, device_id_type=MESH
        )

    wexp_copy = pltpu.make_async_copy(wexp_ref, wexp_v, wexp_sem)
    wexp_copy.start()
    wloc = [
        pltpu.make_async_copy(wout_ref.at[pl.ds(32 * i, 32), :], wbuf.at[2 * z + i], wloc_sem.at[i]) for i in range(2)
    ]
    for copy in wloc:
        copy.start()

    barrier = pltpu.get_barrier_semaphore()
    for k in range(1, 8):
        pl.semaphore_signal(barrier, inc=1, device_id=at_tensor(lax.rem(a + k, NA), z), device_id_type=MESH)
        pl.semaphore_signal(barrier, inc=1, device_id=at_tensor(a, lax.rem(z + k, NZ)), device_id_type=MESH)
        pl.semaphore_signal(barrier, inc=1, device_id={"group": lax.rem(g + k, NG)}, device_id_type=MESH)

    def pack(block, cos, sin):
        rows = block.shape[0]
        lane = iota((rows, 128), 1)
        sin = jnp.where(lane < 32, -sin, sin)
        heads = []
        for j in range(4):
            kb = block[:, 128 * j : 128 * j + 128]
            vb = block[:, 512 + 128 * j : 640 + 128 * j]
            for packed in (
                jnp.where(lane < 64, kb, pltpu.roll(vb, 64, 1)),
                jnp.where(lane < 64, pltpu.roll(kb, 64, 1), vb),
            ):
                swapped = jnp.where(lane < 32, pltpu.roll(packed, 96, 1), pltpu.roll(packed, 32, 1))
                heads.append(packed * cos + swapped * sin)
        return heads

    mine = iota((NA * NZ, 128), 0) == bm_ref[0, 0]
    cos_b = jnp.sum(jnp.where(mine, bcos_ref[...], 0.0), axis=0, keepdims=True)
    sin_b = jnp.sum(jnp.where(mine, bsin_ref[...], 0.0), axis=0, keepdims=True)
    cos_p = cos_b * icos_ref[...] - sin_b * isin_ref[...]
    sin_p = sin_b * icos_ref[...] + cos_b * isin_ref[...]
    stmp[...] = jnp.zeros_like(stmp)
    stmp[0:TOK, :] = sfx_ref[...].astype(F32)
    prefix_heads = pack(pfx_ref[...].astype(F32), cos_p, sin_p)
    quarter = lax.rem(t, 32)
    suffix_heads = pack(stmp[...], scos_ref[quarter], ssin_ref[quarter])
    for h in range(NA):
        kvmsg[h] = jnp.concatenate([prefix_heads[h], suffix_heads[h]], axis=0).astype(BF16)
    kvbuf[z * NA + a] = kvmsg[a]

    swap_row, swap_col = iota((SLOTS, SLOTS), 0), iota((SLOTS, SLOTS), 1)
    swapped_row = ((swap_row >> 2) & 7) * 32 + (swap_row >> 5) * 4 + (swap_row & 3)
    swap = one_hot(swapped_row == swap_col)
    ei, el = iota((64, 128), 0), iota((64, 128), 1)
    q, over_rows = q_ref[...], (((0,), (0,)), ((), ()))
    straight = lax.dot_general(q, one_hot(ei == el), over_rows, preferred_element_type=F32)
    cross = one_hot(((el < 32) & (ei == el + 32)) | ((el >= 32) & (ei == el - 32)))
    crossed = lax.dot_general(q, cross, over_rows, preferred_element_type=F32)
    qlane = iota((SLOTS, 128), 1)
    rotated = straight * qcos_ref[...] + crossed * jnp.where(qlane < 32, -qsin_ref[...], qsin_ref[...])
    rotated = dot(swap, (rotated * 0.125).astype(BF16))
    sink = jnp.broadcast_to(sink_ref[0], (SLOTS, 128))
    s1 = sink.astype(BF16).astype(F32)
    s2 = (sink - s1).astype(BF16).astype(F32)
    s3 = (sink - s1) - s2
    rotated = jnp.where(qlane < 64, rotated, 0.0)
    rotated = jnp.where(qlane == 64, s1, jnp.where(qlane == 65, s2, jnp.where(qlane == 66, s3, rotated)))
    qmsg[...] = rotated.reshape(NZ, ROWS, 128).astype(BF16)
    qbuf[z] = qmsg[z]

    for copy in wloc:
        copy.wait()
    pl.semaphore_wait(barrier, 21)

    def kv_copy(k):
        peer = lax.rem(a + k, NA)
        return remote(kvmsg.at[peer], kvbuf.at[z * NA + a], kv_s.at[k], kv_r.at[a], at_tensor(peer, z))

    def q_copy(k):
        peer = lax.rem(z + k, NZ)
        return remote(qmsg.at[peer], qbuf.at[z], q_s.at[k], q_r.at[z], at_tensor(a, peer))

    for k in range(1, 8):
        kv_copy(k).start()
    for k in range(1, 8):
        q_copy(k).start()

    def kv_ring(direction, k):
        block = lax.rem(z - (k - 1) + NZ, NZ) if direction == 0 else lax.rem(z + (k - 1), NZ)
        first, count = (block * NA, NA) if k < 4 else (block * NA + 4 * direction, 4)
        ref = kvbuf.at[pl.ds(first, count)]
        peer = at_tensor(a, zr if direction == 0 else zl)
        return remote(ref, ref, kvz_s.at[direction, k - 1], kvz_r.at[direction, k - 1], peer)

    def kv_arrived(direction, k):
        block = lax.rem(z - k + NZ, NZ) if direction == 0 else lax.rem(z + k, NZ)
        first, count = (block * NA, NA) if k < 4 else (block * NA + 4 * direction, 4)
        ref = kvbuf.at[pl.ds(first, count)]
        peer = at_tensor(a, zr if direction == 0 else zl)
        return remote(ref, ref, kvz_s.at[direction, k - 1], kvz_r.at[direction, k - 1], peer)

    def w_ref(block, direction, k):
        index = 2 * block + c
        return wbuf.at[index] if k < 4 else wbuf.at[index, pl.ds(16 * direction, 16)]

    def w_ring(direction, k):
        block = lax.rem(z - (k - 1) + NZ, NZ) if direction == 0 else lax.rem(z + (k - 1), NZ)
        ref = w_ref(block, direction, k)
        peer = at_tensor(a, zr if direction == 0 else zl)
        return remote(ref, ref, w_s.at[direction, k - 1], w_r.at[direction, k - 1], peer)

    def w_arrived(direction, k):
        block = lax.rem(z - k + NZ, NZ) if direction == 0 else lax.rem(z + k, NZ)
        ref = w_ref(block, direction, k)
        peer = at_tensor(a, zr if direction == 0 else zl)
        return remote(ref, ref, w_s.at[direction, k - 1], w_r.at[direction, k - 1], peer)

    def w_pass(direction, k):
        block = lax.rem(z - k + NZ, NZ) if direction == 0 else lax.rem(z + k, NZ)
        ref = w_ref(block, direction, k)
        return remote(ref, ref, wp_s.at[direction, k - 1], wp_r.at[direction, k - 1], {"group": mate})

    def w_passed(direction, k):
        block = lax.rem(z - k + NZ, NZ) if direction == 0 else lax.rem(z + k, NZ)
        index = 2 * block + 1 - c
        ref = wbuf.at[index] if k < 4 else wbuf.at[index, pl.ds(16 * direction, 16)]
        return remote(ref, ref, wp_s.at[direction, k - 1], wp_r.at[direction, k - 1], {"group": mate})

    for direction in range(2):
        w_ring(direction, 1).start()

    key_slot = jnp.broadcast_to(keys_ref[0:1, :], (ROWS, KEYS))
    row = iota((ROWS, KEYS), 0)
    own_slot = (row >> 2) * 32 + z * 4 + (row & 3)
    live = jnp.where(own_slot < MAXLEN, len_ref[0, 0], len_ref[0, 1])
    visible = (key_slot < 0) | (
        ((key_slot >> 7) == (own_slot >> 7)) & (key_slot <= own_slot) & ((key_slot & 127) < live)
    )
    bias_ref[...] = jnp.where(visible, 0.0, -1e30)

    pr, pc = iota((64, 128), 0), iota((64, 128), 1)
    gi, gl = iota((NG, 128), 0), iota((NG, 128), 1)
    spread = one_hot(((gl >> 2) & 7) == gi)
    ki, kl = iota((4, 128), 0), iota((4, 128), 1)
    experts = jnp.zeros((4, 128), F32)
    for i in range(TOK):
        experts += jnp.where(
            ((kl & 3) == ki) & ((kl >> 5) == i), dot(routes_ref[i].astype(F32).astype(BF16), spread), 0.0
        )
    experts = jnp.sum(experts, axis=0, keepdims=True)
    named = jnp.broadcast_to(experts, (64, 128)) == (4 * g + ((pr >> 3) & 3)).astype(F32)
    ui, uj = iota((128, 128), 0), iota((128, 128), 1)
    rank = dot(one_hot(named), one_hot(ui < uj))
    wanted = (2 * (pr & 3) + (pr >> 5)).astype(F32)
    hit = one_hot(named & (rank == wanted))
    ti, tj = iota((128, 64), 0), iota((128, 64), 1)
    source = one_hot(((tj >> 3) == ((ti >> 2) & 7)) & ((tj & 3) == (ti >> 5)))
    qr, qc = iota((64, 64), 0), iota((64, 64), 1)
    select = jnp.where(((qr >> 2) & 1) == ((qc >> 2) & 1), dot(hit, source), 0.0).astype(BF16)

    for k in range(1, 8):
        src = lax.rem(a + k, NA)
        remote(kvmsg.at[src], kvbuf.at[z * NA + src], kv_s.at[k], kv_r.at[src], at_tensor(src, z)).wait_recv()
    for direction in range(2):
        kv_ring(direction, 1).start()
    for k in range(1, 5):
        for direction in range(2):
            kv_arrived(direction, k).wait_recv()
            if k < 4:
                kv_ring(direction, k + 1).start()
        if k < 4:
            for direction in range(2):
                w_arrived(direction, k).wait_recv()
                w_ring(direction, k + 1).start()
                w_pass(direction, k).start()

    for k in range(1, 8):
        src = lax.rem(z + k, NZ)
        remote(qmsg.at[src], qbuf.at[src], q_s.at[k], q_r.at[src], at_tensor(a, src)).wait_recv()
    kvb[...] = kvbuf[...].astype(F32).reshape(KEYS, 128).astype(BF16)
    qf = qbuf[...].astype(F32).reshape(SLOTS, 128)
    sinks = jnp.sum(jnp.where((qlane >= 64) & (qlane < 67), qf, 0.0), axis=1, keepdims=True)
    qk = jnp.where(qlane < 64, qf, 0.0).astype(BF16)
    s_ref[...] = dot_t(qk, kvb[...])
    scales = []
    for h in range(NZ):
        rows = slice(ROWS * h, ROWS * h + ROWS)
        scores = s_ref[rows, :] + bias_ref[...]
        sink_h = sinks[rows]
        top = jnp.maximum(jnp.max(scores, axis=1, keepdims=True), sink_h)
        weights = jnp.exp(scores - top)
        scales.append(1.0 / (jnp.sum(weights, axis=1, keepdims=True) + jnp.exp(sink_h - top)))
        p_ref[rows, :] = weights.astype(BF16)
    mixed = dot(p_ref[...], kvb[...]) * jnp.concatenate(scales, axis=0)
    alane = iota((ROWS, 128), 1)
    for j in range(4):
        even, odd = mixed[64 * j : 64 * j + 32], mixed[64 * j + 32 : 64 * j + 64]
        att_ref[:, 128 * j : 128 * j + 128] = jnp.where(alane < 64, pltpu.roll(even, 64, 1), odd).astype(BF16)

    for direction in range(2):
        w_arrived(direction, 4).wait_recv()
        w_pass(direction, 4).start()
    for k in range(1, 5):
        for direction in range(2):
            w_passed(direction, k).wait_recv()

    di, dj = iota((64, ROWS), 0), iota((64, ROWS), 1)
    doubled = dot(one_hot(((di >> 3) * 4 + (di & 3)) == dj), att_ref[...]).astype(BF16)
    weights = wbuf[...].reshape(NZ * 64, D)
    left = dot(doubled, weights[:, :LEFT])
    right = dot(doubled, weights[:, LEFT:])
    half = (iota((64, RIGHT), 0) >> 2) & 1
    rsmsg[:, :, 0:RIGHT] = jnp.where(half == 0, left[:, :RIGHT], right).reshape(NA, 8, RIGHT).astype(BF16)
    rsmsg[:, :, RIGHT:LEFT] = left[:, RIGHT:].reshape(NA, 8, LEFT - RIGHT).astype(BF16)
    rsbuf[a] = rsmsg[a]

    def rs_copy(k):
        peer = lax.rem(a + k, NA)
        return remote(rsmsg.at[peer], rsbuf.at[a], rs_s.at[k], rs_r.at[a], at_tensor(peer, z))

    for k in range(1, 8):
        rs_copy(k).start()
    for k in range(1, 8):
        src = lax.rem(a + k, NA)
        remote(rsmsg.at[src], rsbuf.at[src], rs_s.at[k], rs_r.at[src], at_tensor(src, z)).wait_recv()

    total = rsbuf[0].astype(F32)
    for k in range(1, 8):
        total = total + rsbuf[k].astype(F32)
    tmp[...] = total
    resid = resid_ref[...].astype(F32)
    out_l = (resid[:, :LEFT] + tmp[0:TOK, :]).astype(BF16)
    out_r = (resid[:, LEFT:] + tmp[TOK:8, 0:RIGHT]).astype(BF16)
    ro_ref[:, 0:LEFT] = out_l
    ro_ref[:, LEFT:D] = out_r
    wide_l, wide_r = out_l.astype(F32), out_r.astype(F32)
    square = jnp.sum(wide_l * wide_l, axis=1, keepdims=True) + jnp.sum(wide_r * wide_r, axis=1, keepdims=True)
    scale = lax.rsqrt(square / D + 1e-05)
    tmp[...] = jnp.zeros_like(tmp)
    tmp[0:TOK, :] = wide_l * scale * gain_ref[0:LEFT][None, :]
    tmp[TOK:8, 0:RIGHT] = wide_r * scale * gain_ref[LEFT:D][None, :]
    gmsg[...] = tmp[...].astype(BF16)
    gbuf[g] = gmsg[...]

    def g_copy(k):
        peer = lax.rem(g + k, NG)
        return remote(gmsg, gbuf.at[g], g_s.at[k], g_r.at[g], {"group": peer})

    for k in range(1, 8):
        g_copy(k).start()
    for k in range(1, 8):
        src = lax.rem(g + k, NG)
        remote(gmsg, gbuf.at[src], g_s.at[k], g_r.at[src], {"group": src}).wait_recv()

    pool = gbuf[...].astype(F32).reshape(64, LEFT).astype(BF16)
    dmsg[...] = dot(select, pool).reshape(NA, 8, LEFT).astype(BF16)
    xbuf[z * NA + a] = dmsg[a]

    def d_copy(k):
        peer = lax.rem(a + k, NA)
        return remote(dmsg.at[peer], xbuf.at[z * NA + a], d_s.at[k], d_r.at[a], at_tensor(peer, z))

    for k in range(1, 8):
        d_copy(k).start()

    def x_send(direction, k, j):
        block = lax.rem(z - (k - 1) + NZ, NZ) if direction == 0 else lax.rem(z + (k - 1), NZ)
        ref = xbuf.at[block * NA + j]
        peer = at_tensor(a, zr if direction == 0 else zl)
        return remote(ref, ref, x_s.at[direction, k - 1, j], x_r.at[direction, k - 1, j], peer)

    def x_arrived(direction, k, j):
        block = lax.rem(z - k + NZ, NZ) if direction == 0 else lax.rem(z + k, NZ)
        ref = xbuf.at[block * NA + j]
        peer = at_tensor(a, zr if direction == 0 else zl)
        return remote(ref, ref, x_s.at[direction, k - 1, j], x_r.at[direction, k - 1, j], peer)

    ri, rj = iota((64, 64), 0), iota((64, 64), 1)
    regroup = one_hot(rj == (((ri >> 2) & 7) * 8 + (ri >> 5) * 4 + (ri & 3)))

    def unpack(block):
        plane = xbuf[pl.ds(block * NA, NA)].astype(F32).reshape(64, LEFT).astype(BF16)
        split = dot(regroup, plane).astype(BF16)
        xl[block] = split[0:ROWS]
        xr[block] = split[ROWS:64, 0:RIGHT]

    for k in range(8):
        src = lax.rem(a + k, NA)
        if k > 0:
            remote(dmsg.at[src], xbuf.at[z * NA + src], d_s.at[k], d_r.at[src], at_tensor(src, z)).wait_recv()
        for direction in range(2):
            x_send(direction, 1, src).start()
    unpack(z)
    for k in range(1, 5):
        for i in range(8):
            for direction in range(2):
                if k < 4:
                    j = lax.rem(a + i, NA)
                    x_arrived(direction, k, j).wait_recv()
                    if k < 3:
                        x_send(direction, k + 1, j).start()
                elif i < 4:
                    x_arrived(direction, k, 4 * direction + i).wait_recv()
        if k == 3:
            for i in range(4):
                for direction in range(2):
                    x_send(direction, 4, 4 * direction + i).start()
        unpack(lax.rem(z - k + NZ, NZ))
        if k < 4:
            unpack(lax.rem(z + k, NZ))

    wexp_copy.wait()
    rows_l, rows_r = xl[...].reshape(SLOTS, LEFT), xr[...].reshape(SLOTS, RIGHT)
    gate = dot_t(rows_l, wexp_v[0:PFF, 0:LEFT]) + dot_t(rows_r, wexp_v[0:PFF, LEFT:D])
    up = dot_t(rows_l, wexp_v[PFF:, 0:LEFT]) + dot_t(rows_r, wexp_v[PFF:, LEFT:D])
    gate = jnp.minimum(gate, 7.0)
    up = jnp.clip(up, -7.0, 7.0)
    hidden = ((up + 1.0) * gate * (1.0 / (1.0 + jnp.exp(-1.702 * gate)))).astype(BF16)
    hid_ref[...] = dot(swap, hidden).astype(BF16)

    for k in range(1, 8):
        kv_copy(k).wait_send()
        q_copy(k).wait_send()
        rs_copy(k).wait_send()
        g_copy(k).wait_send()
        d_copy(k).wait_send()
    for direction in range(2):
        for k in range(1, 5):
            kv_ring(direction, k).wait_send()
            w_ring(direction, k).wait_send()
            w_pass(direction, k).wait_send()
            for i in range(8 if k < 4 else 4):
                x_send(direction, k, i if k < 4 else 4 * direction + i).wait_send()


def local(resid_in, queries, suffix_kv, prefix_kv, block_map, lengths, sinks, w_out, mlp_gain, routes, w_experts):
    vmem = pl.BlockSpec(memory_space=pltpu.VMEM)
    smem = pl.BlockSpec(memory_space=pltpu.SMEM)
    hbm = pl.BlockSpec(memory_space=pl.ANY)
    constants = [jnp.asarray(x) for x in tables()]
    dma = pltpu.SemaphoreType.DMA
    resid_out, hidden = pl.pallas_call(
        kernel,
        name="layer",
        out_shape=(jax.ShapeDtypeStruct((TOK, D), BF16), jax.ShapeDtypeStruct((SLOTS, PFF), BF16)),
        in_specs=[vmem, vmem, vmem, smem, smem, smem, vmem, vmem, vmem, hbm, hbm] + [vmem] * len(constants),
        out_specs=(vmem, vmem),
        scratch_shapes=[
            pltpu.VMEM((2 * PFF, D), BF16),
            pltpu.VMEM((2 * NZ, 32, D), BF16),
            pltpu.VMEM((NA, KVR, 128), BF16),
            pltpu.VMEM((NZ * NA, KVR, 128), BF16),
            pltpu.VMEM((NZ, ROWS, 128), BF16),
            pltpu.VMEM((NZ, ROWS, 128), BF16),
            pltpu.VMEM((ROWS, KEYS), F32),
            pltpu.VMEM((KEYS, 128), BF16),
            pltpu.VMEM((SLOTS, KEYS), F32),
            pltpu.VMEM((SLOTS, KEYS), BF16),
            pltpu.VMEM((ROWS, 512), BF16),
            pltpu.VMEM((NA, 8, LEFT), BF16),
            pltpu.VMEM((NA, 8, LEFT), BF16),
            pltpu.VMEM((8, LEFT), F32),
            pltpu.VMEM((SBLK, 1024), F32),
            pltpu.VMEM((8, LEFT), BF16),
            pltpu.VMEM((NG, 8, LEFT), BF16),
            pltpu.VMEM((NA, 8, LEFT), BF16),
            pltpu.VMEM((NZ * NA, 8, LEFT), BF16),
            pltpu.VMEM((NZ, ROWS, LEFT), BF16),
            pltpu.VMEM((NZ, ROWS, RIGHT), BF16),
            dma,
            dma((2,)),
            dma((8,)), dma((8,)),
            dma((2, 4)), dma((2, 4)),
            dma((8,)), dma((8,)),
            dma((2, 4)), dma((2, 4)),
            dma((2, 4)), dma((2, 4)),
            dma((8,)), dma((8,)),
            dma((8,)), dma((8,)),
            dma((8,)), dma((8,)),
            dma((2, 4, 8)), dma((2, 4, 8)),
        ],
        compiler_params=pltpu.CompilerParams(
            collective_id=0, has_side_effects=True, vmem_limit_bytes=60 * 1024 * 1024
        ),
    )(
        jnp.swapaxes(queries, 1, 2)[0], suffix_kv[0], prefix_kv[0], block_map, lengths, sinks, resid_in[0], mlp_gain,
        jnp.swapaxes(routes, 1, 2), w_out, jnp.swapaxes(w_experts, 1, 2)[0], *constants,
    )
    return (resid_out[None], hidden.reshape(1, NA * NZ, TOK, PFF))


def solution(mesh):
    placed = (
        P("group", "tensor", None),
        P("group", None, "tensor"),
        P("group", "tensor", None),
        P("group", "tensor", None),
        P("group", "tensor"),
        P("group", None),
        P("tensor"),
        P("tensor", None),
        P(),
        P("tensor", None, None),
        P(("group", "tensor"), None, None),
    )
    return jax.shard_map(
        local,
        mesh=mesh,
        in_specs=placed,
        out_specs=(P("group", "tensor", None), P(("group", "tensor"), None, None, None)),
        check_vma=False,
    )
```
